32 devices in a mesh: groups: 2 (over y), blk: 4 (over z), win: 4 (over x, core).
Axes of the slice: x: 2, y: 2, z: 4, core: 2. Of those that a mesh axis runs over, the one named last changes fastest.
Arguments:
- spectra: bfloat16 [2, 24, 1024, 201], P(None, 'win', ('groups', 'blk')), parts along dimension 2
- channel_slot: int32 [1024], P(('groups', 'blk')), parts along dimension 0, may hold values from 0 to 511, as said below
- partners: int32 [2, 4], replicated, may hold values from 0 to 3, as said below
Outputs:
- correlations: bfloat16 [2, 1024, 101, 128], P(None, ('groups', 'blk', 'win')), parts along dimension 1
The draws below stay inside these ranges and needn't reach their ends.
There are 2 independent parts, one for each index of `groups`. The reference program is written for one: setup_inputs(seed, part) draws one part's arguments, and reference() takes and returns one part's arrays. A program takes and returns all parts, laid end to end along the dimension named above; an argument that names none is the same for every part. Nothing has to cross between parts.
Inputs may be any that keep to these rules, and one draw needn't show every extreme that they name: channel_slot is a permutation of 0 to 511. For every acquisition shard s (channels s * 128 to s * 128 + 127) and every block b, exactly 32 of the shard's channels go to block b, and they take the slots b * 128 + s * 32 + q for q from 0 to 31. In round r, partners[r, i] = i XOR m_r for one value m_r of 1 to 3 per round; the rounds' values differ.
All inputs are finite; a program needn't handle non-finite values.
Results may differ from the reference program's by a relative error of at most 0.0057.
Values may be sent and summed in bfloat16 or wider, within the bound.
A program may use at most 128 MiB of HBM per device.

```python
import math
import jax
import jax.numpy as jnp
from jax import lax

CH = 128
F = 201
L = 101
ROUNDS = 2
NB = 4
CHANNEL_COUNT = 512
WINDOW_COUNT = 24


def draw_spectra(key, part):
    noise_key = jax.random.fold_in(key, 11)
    transient_event_key = jax.random.fold_in(key, 12)
    colour_key = jax.random.fold_in(key, 13)
    gain_key = jax.random.fold_in(key, 15)
    linear_trend = 3.0 ** (jnp.arange(WINDOW_COUNT, dtype=jnp.float32) / (WINDOW_COUNT - 1))
    transient_event = jnp.exp(jax.random.uniform(transient_event_key, (WINDOW_COUNT, CHANNEL_COUNT), jnp.float32, -math.log(2.0), math.log(2.0)))
    spectral_tint = jnp.exp(jax.random.uniform(colour_key, (CHANNEL_COUNT, F), jnp.float32, math.log(0.3), math.log(3.0)))
    channel_gain = jnp.exp(jax.random.uniform(gain_key, (CHANNEL_COUNT,), jnp.float32, 0.0, math.log(10.0)))
    background_noise = jax.random.normal(noise_key, (2, WINDOW_COUNT, CHANNEL_COUNT, F), jnp.float32)
    value_array = background_noise * linear_trend[None, :, None, None] * transient_event[None, :, :, None] * spectral_tint[None, None, :, :]
    value_array = value_array * channel_gain[None, None, :, None]
    return value_array.astype(jnp.bfloat16)


def draw_channel_slot(key, part):
    per_peer = CH // NB
    keys = jax.random.split(jax.random.fold_in(key, 21), NB)
    orders = jax.vmap(lambda k: jax.random.permutation(k, CH))(keys).astype(jnp.int32)
    shard = jnp.arange(NB, dtype=jnp.int32)[:, None]
    block = orders % NB
    place = orders // NB
    slot = block * CH + shard * per_peer + place
    return slot.reshape(NB * CH).astype(jnp.int32)


def draw_partners(key, part):
    masks = jax.random.permutation(jax.random.fold_in(key, 31), NB - 1)[:ROUNDS].astype(jnp.int32) + 1
    index = jnp.arange(NB, dtype=jnp.int32)
    return jnp.bitwise_xor(index[None, :], masks[:, None]).astype(jnp.int32)


def setup_inputs(seed: int = 0, part: int = 0) -> dict:
    key_of = jax.random.split(jax.random.key(seed), 4)
    part_keys = jax.random.split(jax.random.fold_in(key_of[3], part), 4)
    return {
        "spectra": draw_spectra(jax.random.fold_in(jax.random.fold_in(key_of[3], part), 71), part),
        "channel_slot": draw_channel_slot(jax.random.fold_in(jax.random.fold_in(key_of[3], part), 71), part),
        "partners": draw_partners(jax.random.fold_in(key_of[3], 71), part),
    }


eps_power = 1e-06
half_band = 2

def band_mean(power, windows):
    nbins = power.shape[1]
    padded = jnp.pad(power, ((0, 0), (half_band, half_band)))
    ones = jnp.pad(jnp.ones((nbins,), jnp.float32), (half_band, half_band))
    total = padded[:, 0:nbins]
    count = ones[0:nbins]
    for offset in range(1, 2 * half_band + 1):
        total = total + padded[:, offset:offset + nbins]
        count = count + ones[offset:offset + nbins]
    return total / (count * windows)

def whiten(parts, power, windows):
    scale = lax.rsqrt(band_mean(power, windows) + eps_power)
    return (parts.astype(jnp.float32) * scale).astype(jnp.bfloat16)

def lag_table(nbins, nlags, windows):
    samples = 2 * (nbins - 1)
    freq = jnp.arange(nbins, dtype=jnp.int32)
    lags = jnp.arange(nlags, dtype=jnp.int32) - (nlags - 1) // 2
    phase_index = freq[:, None] * lags[None, :] % samples
    angle = 2.0 * math.pi / samples * phase_index.astype(jnp.float32)
    weight = jnp.where((freq == 0) | (freq == nbins - 1), 1.0, 2.0).astype(jnp.float32)
    norm = 1.0 / math.sqrt(windows * samples)
    cos_part = weight[:, None] * jnp.cos(angle) * norm
    sin_part = -weight[:, None] * jnp.sin(angle) * norm
    return jnp.concatenate([cos_part, sin_part], axis=0)

def correlate(sources, receivers, table):
    left = jnp.concatenate([sources[0], sources[1]], axis=0).astype(jnp.float32)
    turned = jnp.concatenate([sources[1], -sources[0]], axis=0).astype(jnp.float32)
    right = jnp.concatenate([receivers[0], receivers[1]], axis=0).astype(jnp.float32)
    tile = 32
    count = left.shape[1] // tile

    def one_tile(index):
        start = index * tile
        part_left = lax.dynamic_slice_in_dim(left, start, tile, 1)
        part_turned = lax.dynamic_slice_in_dim(turned, start, tile, 1)
        real = jnp.einsum('wak,wbk->kab', part_left, right, precision=lax.Precision.HIGHEST)
        imag = jnp.einsum('wak,wbk->kab', part_turned, right, precision=lax.Precision.HIGHEST)
        stacked = jnp.concatenate([real, imag], axis=0)
        return jnp.einsum('kab,kl->alb', stacked, table, precision=lax.Precision.HIGHEST)
    result = lax.map(one_tile, jnp.arange(count, dtype=jnp.int32))
    return result.reshape(count * tile, table.shape[1], right.shape[1]).astype(jnp.bfloat16)

def reference(spectra, channel_slot, partners):
    blocked = jnp.zeros_like(spectra).at[:, :, channel_slot, :].set(spectra)
    value_array = blocked.astype(jnp.float32)
    power = lax.optimization_barrier(jnp.sum(value_array * value_array, axis=(0, 1)))
    white = whiten(blocked, power, WINDOW_COUNT)
    grouped = white.reshape(2, WINDOW_COUNT, NB, CH, F)
    table = lag_table(F, L, WINDOW_COUNT)
    rounds = []
    for round_index in range(ROUNDS):

        def per_block(index):
            own = lax.dynamic_index_in_dim(grouped, index, 2, keepdims=False)
            other = lax.dynamic_index_in_dim(grouped, partners[round_index, index].astype(jnp.int32), 2, keepdims=False)
            return correlate(own, other, table)
        result = lax.map(per_block, jnp.arange(NB, dtype=jnp.int32))
        rounds.append(result.reshape(NB * CH, L, CH))
    return jnp.stack(rounds, axis=0)
```

```python
import functools
import math

import jax
import jax.numpy as jnp
import numpy as np
from jax import lax
from jax.experimental import pallas as pl
from jax.experimental.pallas import tpu as pltpu
from jax.sharding import PartitionSpec as P

L = 101
ROUNDS = 2


eps_power = 1e-06
half_band = 2
tile_rows = 8


def whiten_into(piece, store, n_win, rows):
    power = None
    for win in range(n_win):
        value_array = piece(win).astype(jnp.float32)
        part = jnp.sum(value_array * value_array, axis=0)
        power = part if power is None else power + part
    nbins = power.shape[1]
    padding = jnp.zeros((power.shape[0], half_band), jnp.float32)
    padded = jnp.concatenate([padding, power, padding], axis=1)
    total = padded[:, 0:nbins]
    for offset in range(1, 2 * half_band + 1):
        total = total + padded[:, offset : offset + nbins]
    place = lax.broadcasted_iota(jnp.int32, power.shape, 1)
    count = 1 + jnp.minimum(place, half_band) + jnp.minimum(nbins - 1 - place, half_band)
    level = total / (count.astype(jnp.float32) * (n_win * rows // 2))
    scale = lax.rsqrt(level + eps_power)
    for win in range(n_win):
        store(win, (piece(win).astype(jnp.float32) * scale).astype(jnp.bfloat16))


def lag_table(nbins, nlags, windows):
    samples = 2 * (nbins - 1)
    freq = jnp.arange(nbins, dtype=jnp.int32)
    lags = jnp.arange(nlags, dtype=jnp.int32) - (nlags - 1) // 2
    phase_index = freq[:, None] * lags[None, :] % samples
    angle = 2.0 * math.pi / samples * phase_index.astype(jnp.float32)
    weight = jnp.where((freq == 0) | (freq == nbins - 1), 1.0, 2.0).astype(jnp.float32)
    norm = 1.0 / math.sqrt(windows * samples)
    cos_part = weight[:, None] * jnp.cos(angle) * norm
    sin_part = -weight[:, None] * jnp.sin(angle) * norm
    return jnp.concatenate([cos_part, sin_part], axis=0)


def correlate(both, right, table):
    cross = jnp.einsum(
        "cwak,wbk->kcab", both, right, preferred_element_type=jnp.float32
    ).astype(jnp.bfloat16)
    return jnp.einsum(
        "kcab,ckl->lab", cross, table, preferred_element_type=jnp.float32
    ).astype(jnp.bfloat16)


def flip(index, bit):
    return index + bit - 2 * bit * ((index // bit) % 2)


def exchange_kernel(
    n_blk, n_win, rounds, pair_ref, own_ref, *refs
):
    right_refs = refs[:rounds]
    both_ref, got_ref, src_ref, pair_send, pair_recv = refs[rounds : rounds + 5]
    pass_send, pass_recv, own_send, own_recv, local_sem = refs[rounds + 5 :]
    blk = lax.axis_index("blk")
    win = lax.axis_index("win")
    per_share = n_blk // n_win
    barrier = pltpu.get_barrier_semaphore()
    for step in range(1, n_blk * n_win):
        other = (blk * n_win + win + step) % (n_blk * n_win)
        pl.semaphore_signal(
            barrier,
            inc=1,
            device_id={"blk": other // n_win, "win": other % n_win},
            device_id_type=pl.DeviceIdType.MESH,
        )
    pl.semaphore_wait(barrier, n_blk * n_win - 1)

    def remote(src, dst, send, recv, to_blk, to_win):
        return pltpu.make_async_remote_copy(
            src_ref=src,
            dst_ref=dst,
            send_sem=send,
            recv_sem=recv,
            device_id={"blk": to_blk, "win": to_win},
            device_id_type=pl.DeviceIdType.MESH,
        )

    bits = []
    bit = n_win // 2
    while bit:
        bits.append(bit)
        bit //= 2

    order = list(range(n_blk))

    def across(step):
        other, each = blk, 1
        while each < n_blk:
            if step & each:
                other = flip(other, each)
            each *= 2
        return other

    def direct(step):
        dest = across(step)
        return remote(
            pair_ref.at[:, :, dest], got_ref.at[:, win, :, blk],
            pair_send.at[step], pair_recv.at[step], dest, win,
        )

    user = blk // per_share
    place = blk % per_share

    def own(step):
        dest = across(step)
        return remote(
            own_ref.at[:, dest], src_ref.at[win, :, place],
            own_send.at[step], own_recv.at[place * n_win + win], dest, user,
        )

    def passed(step, offset, over):
        origin = across(step)
        slot = win
        for each in bits:
            if offset & each:
                slot = flip(slot, each)
        target = got_ref.at[:, slot, :, origin]
        source = pair_ref.at[:, :, blk] if step == 0 and offset == 0 else target
        mark = (offset | over) - 1
        return remote(
            source, target, pass_send.at[mark, step], pass_recv.at[mark, step], blk, flip(win, over)
        )

    rows = pair_ref.shape[1]
    half = rows // 2
    keep = pltpu.make_async_copy(
        pair_ref.at[:, :, blk], got_ref.at[:, win, :, blk], local_sem.at[0]
    )
    keep.start()
    is_user = user == win

    def own_keep():
        return pltpu.make_async_copy(
            own_ref.at[:, blk], src_ref.at[win, :, place], local_sem.at[1]
        )

    @pl.when(is_user)
    def _():
        own_keep().start()

    passes = []
    held = [0]
    for over in bits:
        passes.extend((offset, over) for offset in held)
        held = held + [offset | over for offset in held]

    sends = []
    for offset, over in passes:
        if offset == 0:
            copy = passed(0, 0, over)
            copy.start()
            sends.append(copy)
    for step in order[1:]:
        copy = direct(step)
        copy.start()
        sends.append(copy)
    for step in order[1:]:
        copy = own(step)
        copy.start()
        sends.append(copy)

    @pl.when(jnp.logical_not(is_user))
    def _():
        own(0).start()

    keep.wait()

    @pl.when(is_user)
    def _():
        own_keep().wait()

    waited = set()

    def arrive(step, offset):
        if (step, offset) in waited:
            return
        waited.add((step, offset))
        if offset == 0:
            if step:
                direct(step).wait_recv()
        else:
            over = offset & -offset
            passed(step, offset - over, over).wait_recv()

    def finish(step):
        for offset in held:
            arrive(step, offset)
        origin = across(step)

        for index in range(rounds):

            def store(peer, white):
                right_refs[index][pl.ds(peer * rows, rows), origin] = white

            whiten_into(lambda peer: got_ref[index, peer, :, origin], store, n_win, rows)

    for turn in range(n_blk + 1):
        if 1 <= turn < n_blk:
            step = order[turn]
            arrive(step, 0)
            for offset, over in passes:
                if offset == 0:
                    copy = passed(step, 0, over)
                    copy.start()
                    sends.append(copy)
        if turn >= 1:
            step = order[turn - 1]
            for offset, over in passes:
                if offset:
                    arrive(step, offset)
                    copy = passed(step, offset, over)
                    copy.start()
                    sends.append(copy)
        if turn >= 2:
            finish(order[turn - 2])
    finish(order[n_blk - 1])
    for local in range(per_share):
        for peer in range(n_win):
            here = jnp.logical_and(blk == win * per_share + local, win == peer)

            @pl.when(jnp.logical_not(here))
            def _():
                piece = src_ref.at[peer, :, local]
                remote(
                    piece, piece, own_send.at[0], own_recv.at[local * n_win + peer], blk, win
                ).wait_recv()

    def one_shard(local, carry):
        def store(peer, white):
            both_ref[0, pl.ds(peer * rows, rows), local] = white
            both_ref[1, pl.ds(peer * rows, half), local] = white[half:]
            both_ref[1, pl.ds(peer * rows + half, half), local] = -white[:half]

        whiten_into(lambda peer: src_ref[peer, :, local], store, n_win, rows)
        return carry

    lax.fori_loop(0, per_share, one_shard, 0)

    for copy in sends:
        copy.wait_send()

    @pl.when(jnp.logical_not(is_user))
    def _():
        own(0).wait_send()


def exchange(pair, own, n_blk, n_win):
    rounds, rows, _, per_peer, nbins = pair.shape
    per_share = n_blk // n_win
    dtype = pair.dtype
    anywhere = pl.BlockSpec(memory_space=pl.ANY)
    vmem = pl.BlockSpec(memory_space=pltpu.VMEM)
    depth = n_win * rows
    return pl.pallas_call(
        functools.partial(exchange_kernel, n_blk, n_win, rounds),
        out_shape=(
            *[jax.ShapeDtypeStruct((depth, n_blk, per_peer, nbins), dtype)] * rounds,
            jax.ShapeDtypeStruct((2, depth, per_share, per_peer, nbins), dtype),
        ),
        in_specs=[anywhere, anywhere],
        out_specs=(vmem,) * (rounds + 1),
        scratch_shapes=[
            pltpu.VMEM((rounds, n_win, rows, n_blk, per_peer, nbins), dtype),
            pltpu.VMEM((n_win, rows, per_share, per_peer, nbins), dtype),
            pltpu.SemaphoreType.DMA((n_blk,)),
            pltpu.SemaphoreType.DMA((n_blk,)),
            pltpu.SemaphoreType.DMA((n_win - 1, n_blk)),
            pltpu.SemaphoreType.DMA((n_win - 1, n_blk)),
            pltpu.SemaphoreType.DMA((n_blk,)),
            pltpu.SemaphoreType.DMA((n_blk,)),
            pltpu.SemaphoreType.DMA((2,)),
        ],
        compiler_params=pltpu.CompilerParams(collective_id=0, has_side_effects=True),
    )(pair, own)


def plain_body(spectra, channel_slot, partners):
    n_blk = lax.axis_size("blk")
    n_win = lax.axis_size("win")
    parts, mine, chans, nbins = spectra.shape
    rows = parts * mine
    per_peer = chans // n_blk
    here = lax.axis_index("blk")
    share = chans // n_win
    windows = mine * n_win
    flat = spectra.reshape(rows, chans, nbins)
    wanted = jnp.concatenate([partners, jnp.arange(n_blk, dtype=jnp.int32)[None]], axis=0)
    slots = (
        wanted[:, :, None] * chans
        + here * per_peer
        + jnp.arange(per_peer, dtype=jnp.int32)[None, None, :]
    )
    selector = (slots[..., None] == channel_slot).astype(jnp.bfloat16)
    pair = jnp.einsum(
        "tzqc,xcf->txzqf", selector[:ROUNDS], flat, preferred_element_type=jnp.float32
    ).astype(jnp.bfloat16)
    own = jnp.einsum(
        "zqc,xcf->xzqf", selector[ROUNDS], flat, preferred_element_type=jnp.float32
    ).astype(jnp.bfloat16)
    *right, both = exchange(pair, own, n_blk, n_win)
    right = [each.reshape(n_win * rows, chans, nbins) for each in right]
    both = both.reshape(2, n_win * rows, share, nbins)
    table = lag_table(nbins, L, windows).reshape(2, nbins, L).astype(jnp.bfloat16)
    results = [correlate(both, right[index], table) for index in range(ROUNDS)]
    return jnp.stack(results, axis=0).transpose(0, 2, 1, 3)


def select_kernel(n_blk, slots_ref, partners_ref, x_ref, out_ref):
    dest = pl.program_id(0)
    here = lax.axis_index("blk")
    parts, _, nbins, chans = x_ref.shape
    kinds, groups = out_ref.shape[1], out_ref.shape[2]
    per_peer = chans // n_blk
    row = lax.broadcasted_iota(jnp.int32, (chans, chans), 0)
    slots = slots_ref[...]
    picks = []
    for kind in range(kinds):
        block = dest if kind == kinds - 1 else partners_ref[kind, dest]
        hit = slots == block * chans + here * per_peer + row % per_peer
        picks.append(
            jnp.concatenate(
                [
                    jnp.where(hit & (row // per_peer == y), 1.0, 0.0).astype(jnp.bfloat16)
                    for y in range(n_blk)
                ],
                axis=1,
            )
        )
    pick = jnp.concatenate(picks, axis=0)
    for group in range(groups):
        rows = [divmod(group * n_blk + y, parts) for y in range(n_blk)]
        wide = jnp.concatenate([x_ref[part, win] for win, part in rows], axis=1)
        got = lax.dot_general(
            wide, pick, (((1,), (1,)), ((), ())), preferred_element_type=jnp.float32
        ).astype(jnp.bfloat16)
        for kind in range(kinds):
            out_ref[0, kind, group] = got[:, kind * chans : (kind + 1) * chans]


def select(flat, slots, partners, n_blk, kinds):
    parts, mine, nbins, chans = flat.shape
    groups = parts * mine // n_blk
    return pl.pallas_call(
        functools.partial(select_kernel, n_blk),
        grid=(n_blk,),
        out_shape=jax.ShapeDtypeStruct((n_blk, kinds, groups, nbins, chans), flat.dtype),
        in_specs=[
            pl.BlockSpec((1, chans), lambda d: (0, 0)),
            pl.BlockSpec(memory_space=pltpu.SMEM),
            pl.BlockSpec(flat.shape, lambda d: (0, 0, 0, 0)),
        ],
        out_specs=pl.BlockSpec((1, kinds, groups, nbins, chans), lambda d: (d, 0, 0, 0, 0)),
    )(slots, partners, flat)


def across(index, step, count):
    other, bit = index, 1
    while bit < count:
        if step & bit:
            other = flip(other, bit)
        bit *= 2
    return other


def spread_kernel(
    n, rounds, piece_ref, got_ref, own_ref, stage_ref,
    far_send, far_recv, stage_send, stage_recv, pass_send, pass_recv,
    own_send, own_recv, local_sem,
):
    blk = lax.axis_index("blk")
    win = lax.axis_index("win")

    def remote(src, dst, send, recv, to_blk, to_win):
        return pltpu.make_async_remote_copy(
            src_ref=src,
            dst_ref=dst,
            send_sem=send,
            recv_sem=recv,
            device_id={"blk": to_blk, "win": to_win},
            device_id_type=pl.DeviceIdType.MESH,
        )

    barrier = pltpu.get_barrier_semaphore()
    for step in range(1, n):
        for to_blk, to_win in ((across(blk, step, n), win), (blk, across(win, step, n))):
            pl.semaphore_signal(
                barrier,
                inc=1,
                device_id={"blk": to_blk, "win": to_win},
                device_id_type=pl.DeviceIdType.MESH,
            )

    def far(turn, step):
        dest = across(blk, step, n)
        return remote(
            piece_ref.at[dest, turn], got_ref.at[turn, blk, win],
            far_send.at[turn, step], far_recv.at[turn, step], dest, win,
        )

    def staged(step):
        dest = across(blk, step, n)
        return remote(
            piece_ref.at[dest, rounds], stage_ref.at[blk],
            stage_send.at[step], stage_recv.at[blk], dest, win,
        )

    def own(step):
        user = across(win, step, n)
        return remote(
            stage_ref.at[user], own_ref.at[win], own_send.at[step], own_recv.at[step], blk, user
        )

    bits = []
    bit = n // 2
    while bit:
        bits.append(bit)
        bit //= 2
    passes = []
    held = [0]
    for over in bits:
        passes.extend((offset, over) for offset in held)
        held = held + [offset | over for offset in held]

    def passed(turn, step, offset, over):
        origin = across(blk, step, n)
        piece = got_ref.at[turn, origin, across(win, offset, n)]
        source = piece_ref.at[blk, turn] if step == 0 and offset == 0 else piece
        mark = (offset | over) - 1
        return remote(
            source, piece, pass_send.at[turn, step, mark], pass_recv.at[turn, step, mark],
            blk, flip(win, over),
        )

    sends = []

    def go(copy):
        copy.start()
        sends.append(copy)

    keeps = [
        pltpu.make_async_copy(
            piece_ref.at[blk, turn], got_ref.at[turn, blk, win], local_sem.at[turn]
        )
        for turn in range(rounds)
    ]
    home = pltpu.make_async_copy(piece_ref.at[blk, rounds], stage_ref.at[blk], stage_recv.at[blk])
    for keep in keeps:
        keep.start()
    home.start()
    pl.semaphore_wait(barrier, 2 * (n - 1))
    steps = list(range(n - 1, 0, -1))
    for step in steps:
        go(far(0, step))
    for offset, over in passes:
        if offset == 0:
            go(passed(0, 0, 0, over))
    for step in steps:
        go(staged(step))
    for step in steps:
        go(far(1, step))
    for turn in range(1, rounds):
        for offset, over in passes:
            if offset == 0:
                go(passed(turn, 0, 0, over))

    waited = set()

    def arrive(turn, step, offset):
        if (turn, step, offset) in waited:
            return
        waited.add((turn, step, offset))
        if offset == 0:
            if step:
                far(turn, step).wait_recv()
        else:
            over = offset & -offset
            passed(turn, step, offset - over, over).wait_recv()

    def onward(turn, step, first):
        for offset, over in passes:
            if (offset == 0) == first:
                arrive(turn, step, offset)
                go(passed(turn, step, offset, over))

    order = [0] + list(range(1, n))
    for turn in range(rounds):
        for place, step in enumerate(order):
            if step:
                onward(turn, step, True)
            if place:
                onward(turn, order[place - 1], False)
        onward(turn, order[-1], False)
        if turn == 0:
            for step in range(1, n):
                user = across(win, step, n)
                piece = stage_ref.at[user]
                pltpu.make_async_copy(piece, piece, stage_recv.at[user]).wait()
                go(own(step))
            piece = stage_ref.at[win]
            pltpu.make_async_copy(piece, piece, stage_recv.at[win]).wait()
            mine = pltpu.make_async_copy(piece, own_ref.at[win], local_sem.at[rounds])
            mine.start()
    for turn in range(rounds):
        for step in order:
            for offset in held:
                arrive(turn, step, offset)
    for step in range(1, n):
        own(step).wait_recv()
    mine.wait()
    for keep in keeps:
        keep.wait()
    for copy in sends:
        copy.wait_send()


def spread(pieces, n, rounds):
    shape, dtype = pieces.shape[2:], pieces.dtype
    anywhere = pl.BlockSpec(memory_space=pl.ANY)
    dma = pltpu.SemaphoreType.DMA
    got, own, _ = pl.pallas_call(
        functools.partial(spread_kernel, n, rounds),
        out_shape=(
            jax.ShapeDtypeStruct((rounds, n, n, *shape), dtype),
            jax.ShapeDtypeStruct((n, *shape), dtype),
            jax.ShapeDtypeStruct((n, *shape), dtype),
        ),
        in_specs=[anywhere],
        out_specs=(anywhere,) * 3,
        scratch_shapes=[
            dma((rounds, n)), dma((rounds, n)), dma((n,)), dma((n,)),
            dma((rounds, n, n - 1)), dma((rounds, n, n - 1)), dma((n,)), dma((n,)),
            dma((rounds + 1,)),
        ],
        compiler_params=pltpu.CompilerParams(collective_id=1, has_side_effects=True),
    )(pieces)
    return got, own


def lane_spread(n, per_peer, chans):
    regroup = np.zeros((n, n, per_peer, n, n, per_peer), np.float32)
    for shard in range(n):
        for y in range(n):
            for q in range(per_peer):
                regroup[shard, y, q, y, shard, q] = 1.0
    turned = np.zeros((n, per_peer, n, chans), np.float32)
    for y in range(n):
        for q in range(per_peer):
            turned[y, q, y, q] = 1.0
            part = y % 2
            turned[y + 1 - 2 * part, q, y, per_peer + q] = 1.0 if part == 0 else -1.0
    return regroup.reshape(n * chans, n * chans), turned.reshape(chans, n * chans)


def combine_kernel(
    n, unroll, got_ref, own_ref, regroup_ref, turn_ref, table_ref, out_ref,
    right_ref, left_ref, cross_ref, pad_ref, scale_ref,
):
    rounds, _, _, groups, nbins, chans = got_ref.shape
    per_peer = chans // n
    depth = n * groups * n
    stride = right_ref.shape[1] // depth
    pad = (pad_ref.shape[0] - stride) // 2
    pad_ref[...] = jnp.zeros_like(pad_ref)
    place = lax.broadcasted_iota(jnp.int32, (nbins, chans), 0)
    count = 1 + jnp.minimum(place, half_band) + jnp.minimum(nbins - 1 - place, half_band)
    weight = 1.0 / (count.astype(jnp.float32) * (depth // 2))

    def scale_of(piece):
        def add(index, total):
            value = piece(index // groups, index % groups).astype(jnp.float32)
            return total + value * value

        power = lax.fori_loop(0, n * groups, add, jnp.zeros((nbins, chans), jnp.float32))
        total = power
        for y in range(1, n):
            total = total + pltpu.roll(power, y * per_peer, 1)
        pad_ref[pl.ds(pad, nbins)] = total
        near = pad_ref[pl.ds(pad - half_band, nbins)]
        for offset in range(1 - half_band, half_band + 1):
            near = near + pad_ref[pl.ds(pad + offset, nbins)]
        return lax.rsqrt(near * weight + eps_power)

    scale_ref[0] = scale_of(lambda win, group: own_ref[win, group])

    def place_left(index, carry):
        win, group = index // groups, index % groups
        white = (own_ref[win, group].astype(jnp.float32) * scale_ref[0]).astype(jnp.bfloat16)
        wide = jnp.dot(white, turn_ref[...], preferred_element_type=jnp.float32)
        for y in range(n):
            left_ref[pl.ds((index * n + y) * stride, nbins)] = wide[:, y * chans : (y + 1) * chans]
        return carry

    lax.fori_loop(0, n * groups, place_left, 0)

    for turn in range(rounds):
        for shard in range(n):
            scale_ref[shard] = scale_of(lambda win, group: got_ref[turn, shard, win, group])

        def place_right(index, carry):
            win, group = index // groups, index % groups
            white = jnp.concatenate(
                [
                    (got_ref[turn, shard, win, group].astype(jnp.float32) * scale_ref[shard]).astype(
                        jnp.bfloat16
                    )
                    for shard in range(n)
                ],
                axis=1,
            )
            wide = jnp.dot(white, regroup_ref[...], preferred_element_type=jnp.float32)
            for y in range(n):
                right_ref[turn, pl.ds((index * n + y) * stride, nbins)] = wide[
                    :, y * chans : (y + 1) * chans
                ]
            return carry

        lax.fori_loop(0, n * groups, place_right, 0)

    both = 2 * per_peer

    def one_bin(bin_index):
        left = left_ref[pl.ds(bin_index, depth, stride)].astype(jnp.bfloat16)
        right = jnp.concatenate(
            [
                right_ref[turn, pl.ds(bin_index, depth, stride)].astype(jnp.bfloat16)
                for turn in range(rounds)
            ],
            axis=1,
        )
        cross = lax.dot_general(
            left, right, (((0,), (0,)), ((), ())), preferred_element_type=jnp.float32
        )
        for turn in range(rounds):
            cross_ref[turn, pl.ds(bin_index * both, both)] = cross[
                :both, turn * chans : (turn + 1) * chans
            ]

    def some_bins(index, carry):
        for offset in range(unroll):
            one_bin(index * unroll + offset)
        return carry

    lax.fori_loop(0, nbins // unroll, some_bins, 0)
    for bin_index in range(nbins // unroll * unroll, nbins):
        one_bin(bin_index)

    def one_source(source):
        total = None
        for part in range(2):
            rows = jnp.concatenate(
                [
                    cross_ref[turn, pl.ds(part * per_peer + source, nbins, both)].astype(jnp.bfloat16)
                    for turn in range(rounds)
                ],
                axis=1,
            )
            term = jnp.dot(table_ref[part], rows, preferred_element_type=jnp.float32)
            total = term if total is None else total + term
        total = total.astype(jnp.bfloat16)
        for turn in range(rounds):
            out_ref[turn, source] = total[:, turn * chans : (turn + 1) * chans]

    def two_sources(index, carry):
        one_source(2 * index)
        one_source(2 * index + 1)
        return carry

    lax.fori_loop(0, per_peer // 2, two_sources, 0)


def combine(got, own, n, windows):
    rounds, _, _, groups, nbins, chans = got.shape
    per_peer = chans // n
    depth = n * groups * n
    stride = (nbins + 7) // 8 * 8
    regroup, turned = lane_spread(n, per_peer, chans)
    table = fixed_table(nbins, L, windows)
    vmem = pl.BlockSpec(memory_space=pltpu.VMEM)
    return pl.pallas_call(
        functools.partial(combine_kernel, n, 8),
        out_shape=jax.ShapeDtypeStruct((rounds, per_peer, L, chans), jnp.bfloat16),
        in_specs=[vmem] * 5,
        out_specs=vmem,
        scratch_shapes=[
            pltpu.VMEM((rounds, depth * stride, chans), jnp.float32),
            pltpu.VMEM((depth * stride, chans), jnp.float32),
            pltpu.VMEM((rounds, nbins * 2 * per_peer, chans), jnp.float32),
            pltpu.VMEM((stride + 16, chans), jnp.float32),
            pltpu.VMEM((n, nbins, chans), jnp.float32),
        ],
    )(
        got, own, jnp.asarray(regroup, jnp.bfloat16), jnp.asarray(turned, jnp.bfloat16),
        jnp.asarray(table, jnp.bfloat16),
    )


def fixed_table(nbins, nlags, windows):
    samples = 2 * (nbins - 1)
    freq = np.arange(nbins)
    lags = np.arange(nlags) - (nlags - 1) // 2
    angle = 2.0 * np.pi / samples * (lags[:, None] * freq[None, :] % samples)
    weight = np.where((freq == 0) | (freq == nbins - 1), 1.0, 2.0) / np.sqrt(windows * samples)
    return np.stack([np.cos(angle) * weight, -np.sin(angle) * weight]).astype(np.float32)


def dense_body(spectra, channel_slot, partners):
    n = lax.axis_size("blk")
    parts, mine, chans, nbins = spectra.shape
    rounds = partners.shape[0]
    flat = spectra.transpose(0, 1, 3, 2)
    pieces = select(flat, channel_slot.reshape(1, chans), partners, n, rounds + 1)
    got, own = spread(pieces, n, rounds)
    return combine(got, own, n, mine * n)


def body(spectra, channel_slot, partners):
    n_blk = lax.axis_size("blk")
    rows = spectra.shape[0] * spectra.shape[1]
    fits = n_blk == lax.axis_size("win") and rows % n_blk == 0 and n_blk % spectra.shape[0] == 0
    if fits and 2 * spectra.shape[2] // n_blk <= spectra.shape[2]:
        return dense_body(spectra, channel_slot, partners)
    return plain_body(spectra, channel_slot, partners)


def solution(mesh):
    in_specs = (P(None, "win", ("groups", "blk"), None), P(("groups", "blk")), P())
    out_specs = P(None, ("groups", "blk", "win"), None, None)
    return jax.shard_map(body, mesh=mesh, in_specs=in_specs, out_specs=out_specs, check_vma=False)
```

```python
import functools
import math

import jax
import jax.numpy as jnp
import numpy as np
from jax import lax
from jax.experimental import pallas as pl
from jax.experimental.pallas import tpu as pltpu
from jax.sharding import PartitionSpec as P

L = 101
ROUNDS = 2


eps_power = 1e-06
half_band = 2
tile_rows = 8


def whiten_into(piece, store, n_win, rows):
    power = None
    for win in range(n_win):
        value_array = piece(win).astype(jnp.float32)
        part = jnp.sum(value_array * value_array, axis=0)
        power = part if power is None else power + part
    nbins = power.shape[1]
    padding = jnp.zeros((power.shape[0], half_band), jnp.float32)
    padded = jnp.concatenate([padding, power, padding], axis=1)
    total = padded[:, 0:nbins]
    for offset in range(1, 2 * half_band + 1):
        total = total + padded[:, offset : offset + nbins]
    place = lax.broadcasted_iota(jnp.int32, power.shape, 1)
    count = 1 + jnp.minimum(place, half_band) + jnp.minimum(nbins - 1 - place, half_band)
    level = total / (count.astype(jnp.float32) * (n_win * rows // 2))
    scale = lax.rsqrt(level + eps_power)
    for win in range(n_win):
        store(win, (piece(win).astype(jnp.float32) * scale).astype(jnp.bfloat16))


def lag_table(nbins, nlags, windows):
    samples = 2 * (nbins - 1)
    freq = jnp.arange(nbins, dtype=jnp.int32)
    lags = jnp.arange(nlags, dtype=jnp.int32) - (nlags - 1) // 2
    phase_index = freq[:, None] * lags[None, :] % samples
    angle = 2.0 * math.pi / samples * phase_index.astype(jnp.float32)
    weight = jnp.where((freq == 0) | (freq == nbins - 1), 1.0, 2.0).astype(jnp.float32)
    norm = 1.0 / math.sqrt(windows * samples)
    cos_part = weight[:, None] * jnp.cos(angle) * norm
    sin_part = -weight[:, None] * jnp.sin(angle) * norm
    return jnp.concatenate([cos_part, sin_part], axis=0)


def correlate(both, right, table):
    cross = jnp.einsum(
        "cwak,wbk->kcab", both, right, preferred_element_type=jnp.float32
    ).astype(jnp.bfloat16)
    return jnp.einsum(
        "kcab,ckl->lab", cross, table, preferred_element_type=jnp.float32
    ).astype(jnp.bfloat16)


def flip(index, bit):
    return index + bit - 2 * bit * ((index // bit) % 2)


def exchange_kernel(
    n_blk, n_win, rounds, pair_ref, own_ref, *refs
):
    right_refs = refs[:rounds]
    both_ref, got_ref, src_ref, pair_send, pair_recv = refs[rounds : rounds + 5]
    pass_send, pass_recv, own_send, own_recv, local_sem = refs[rounds + 5 :]
    blk = lax.axis_index("blk")
    win = lax.axis_index("win")
    per_share = n_blk // n_win
    barrier = pltpu.get_barrier_semaphore()
    for step in range(1, n_blk * n_win):
        other = (blk * n_win + win + step) % (n_blk * n_win)
        pl.semaphore_signal(
            barrier,
            inc=1,
            device_id={"blk": other // n_win, "win": other % n_win},
            device_id_type=pl.DeviceIdType.MESH,
        )
    pl.semaphore_wait(barrier, n_blk * n_win - 1)

    def remote(src, dst, send, recv, to_blk, to_win):
        return pltpu.make_async_remote_copy(
            src_ref=src,
            dst_ref=dst,
            send_sem=send,
            recv_sem=recv,
            device_id={"blk": to_blk, "win": to_win},
            device_id_type=pl.DeviceIdType.MESH,
        )

    bits = []
    bit = n_win // 2
    while bit:
        bits.append(bit)
        bit //= 2

    order = list(range(n_blk))

    def across(step):
        other, each = blk, 1
        while each < n_blk:
            if step & each:
                other = flip(other, each)
            each *= 2
        return other

    def direct(step):
        dest = across(step)
        return remote(
            pair_ref.at[:, :, dest], got_ref.at[:, win, :, blk],
            pair_send.at[step], pair_recv.at[step], dest, win,
        )

    user = blk // per_share
    place = blk % per_share

    def own(step):
        dest = across(step)
        return remote(
            own_ref.at[:, dest], src_ref.at[win, :, place],
            own_send.at[step], own_recv.at[place * n_win + win], dest, user,
        )

    def passed(step, offset, over):
        origin = across(step)
        slot = win
        for each in bits:
            if offset & each:
                slot = flip(slot, each)
        target = got_ref.at[:, slot, :, origin]
        source = pair_ref.at[:, :, blk] if step == 0 and offset == 0 else target
        mark = (offset | over) - 1
        return remote(
            source, target, pass_send.at[mark, step], pass_recv.at[mark, step], blk, flip(win, over)
        )

    rows = pair_ref.shape[1]
    half = rows // 2
    keep = pltpu.make_async_copy(
        pair_ref.at[:, :, blk], got_ref.at[:, win, :, blk], local_sem.at[0]
    )
    keep.start()
    is_user = user == win

    def own_keep():
        return pltpu.make_async_copy(
            own_ref.at[:, blk], src_ref.at[win, :, place], local_sem.at[1]
        )

    @pl.when(is_user)
    def _():
        own_keep().start()

    passes = []
    held = [0]
    for over in bits:
        passes.extend((offset, over) for offset in held)
        held = held + [offset | over for offset in held]

    sends = []
    for offset, over in passes:
        if offset == 0:
            copy = passed(0, 0, over)
            copy.start()
            sends.append(copy)
    for step in order[1:]:
        copy = direct(step)
        copy.start()
        sends.append(copy)
    for step in order[1:]:
        copy = own(step)
        copy.start()
        sends.append(copy)

    @pl.when(jnp.logical_not(is_user))
    def _():
        own(0).start()

    keep.wait()

    @pl.when(is_user)
    def _():
        own_keep().wait()

    waited = set()

    def arrive(step, offset):
        if (step, offset) in waited:
            return
        waited.add((step, offset))
        if offset == 0:
            if step:
                direct(step).wait_recv()
        else:
            over = offset & -offset
            passed(step, offset - over, over).wait_recv()

    def finish(step):
        for offset in held:
            arrive(step, offset)
        origin = across(step)

        for index in range(rounds):

            def store(peer, white):
                right_refs[index][pl.ds(peer * rows, rows), origin] = white

            whiten_into(lambda peer: got_ref[index, peer, :, origin], store, n_win, rows)

    for turn in range(n_blk + 1):
        if 1 <= turn < n_blk:
            step = order[turn]
            arrive(step, 0)
            for offset, over in passes:
                if offset == 0:
                    copy = passed(step, 0, over)
                    copy.start()
                    sends.append(copy)
        if turn >= 1:
            step = order[turn - 1]
            for offset, over in passes:
                if offset:
                    arrive(step, offset)
                    copy = passed(step, offset, over)
                    copy.start()
                    sends.append(copy)
        if turn >= 2:
            finish(order[turn - 2])
    finish(order[n_blk - 1])
    for local in range(per_share):
        for peer in range(n_win):
            here = jnp.logical_and(blk == win * per_share + local, win == peer)

            @pl.when(jnp.logical_not(here))
            def _():
                piece = src_ref.at[peer, :, local]
                remote(
                    piece, piece, own_send.at[0], own_recv.at[local * n_win + peer], blk, win
                ).wait_recv()

    def one_shard(local, carry):
        def store(peer, white):
            both_ref[0, pl.ds(peer * rows, rows), local] = white
            both_ref[1, pl.ds(peer * rows, half), local] = white[half:]
            both_ref[1, pl.ds(peer * rows + half, half), local] = -white[:half]

        whiten_into(lambda peer: src_ref[peer, :, local], store, n_win, rows)
        return carry

    lax.fori_loop(0, per_share, one_shard, 0)

    for copy in sends:
        copy.wait_send()

    @pl.when(jnp.logical_not(is_user))
    def _():
        own(0).wait_send()


def exchange(pair, own, n_blk, n_win):
    rounds, rows, _, per_peer, nbins = pair.shape
    per_share = n_blk // n_win
    dtype = pair.dtype
    anywhere = pl.BlockSpec(memory_space=pl.ANY)
    vmem = pl.BlockSpec(memory_space=pltpu.VMEM)
    depth = n_win * rows
    return pl.pallas_call(
        functools.partial(exchange_kernel, n_blk, n_win, rounds),
        out_shape=(
            *[jax.ShapeDtypeStruct((depth, n_blk, per_peer, nbins), dtype)] * rounds,
            jax.ShapeDtypeStruct((2, depth, per_share, per_peer, nbins), dtype),
        ),
        in_specs=[anywhere, anywhere],
        out_specs=(vmem,) * (rounds + 1),
        scratch_shapes=[
            pltpu.VMEM((rounds, n_win, rows, n_blk, per_peer, nbins), dtype),
            pltpu.VMEM((n_win, rows, per_share, per_peer, nbins), dtype),
            pltpu.SemaphoreType.DMA((n_blk,)),
            pltpu.SemaphoreType.DMA((n_blk,)),
            pltpu.SemaphoreType.DMA((n_win - 1, n_blk)),
            pltpu.SemaphoreType.DMA((n_win - 1, n_blk)),
            pltpu.SemaphoreType.DMA((n_blk,)),
            pltpu.SemaphoreType.DMA((n_blk,)),
            pltpu.SemaphoreType.DMA((2,)),
        ],
        compiler_params=pltpu.CompilerParams(collective_id=0, has_side_effects=True),
    )(pair, own)


def plain_body(spectra, channel_slot, partners):
    n_blk = lax.axis_size("blk")
    n_win = lax.axis_size("win")
    parts, mine, chans, nbins = spectra.shape
    rows = parts * mine
    per_peer = chans // n_blk
    here = lax.axis_index("blk")
    share = chans // n_win
    windows = mine * n_win
    flat = spectra.reshape(rows, chans, nbins)
    wanted = jnp.concatenate([partners, jnp.arange(n_blk, dtype=jnp.int32)[None]], axis=0)
    slots = (
        wanted[:, :, None] * chans
        + here * per_peer
        + jnp.arange(per_peer, dtype=jnp.int32)[None, None, :]
    )
    selector = (slots[..., None] == channel_slot).astype(jnp.bfloat16)
    pair = jnp.einsum(
        "tzqc,xcf->txzqf", selector[:ROUNDS], flat, preferred_element_type=jnp.float32
    ).astype(jnp.bfloat16)
    own = jnp.einsum(
        "zqc,xcf->xzqf", selector[ROUNDS], flat, preferred_element_type=jnp.float32
    ).astype(jnp.bfloat16)
    *right, both = exchange(pair, own, n_blk, n_win)
    right = [each.reshape(n_win * rows, chans, nbins) for each in right]
    both = both.reshape(2, n_win * rows, share, nbins)
    table = lag_table(nbins, L, windows).reshape(2, nbins, L).astype(jnp.bfloat16)
    results = [correlate(both, right[index], table) for index in range(ROUNDS)]
    return jnp.stack(results, axis=0).transpose(0, 2, 1, 3)


def select_kernel(n_blk, slots_ref, partners_ref, x_ref, out_ref):
    dest = pl.program_id(0)
    here = lax.axis_index("blk")
    parts, _, nbins, chans = x_ref.shape
    kinds, groups = out_ref.shape[1], out_ref.shape[2]
    per_peer = chans // n_blk
    row = lax.broadcasted_iota(jnp.int32, (chans, chans), 0)
    slots = slots_ref[...]
    picks = []
    for kind in range(kinds):
        block = dest if kind == kinds - 1 else partners_ref[kind, dest]
        hit = slots == block * chans + here * per_peer + row % per_peer
        picks.append(
            jnp.concatenate(
                [
                    jnp.where(hit & (row // per_peer == y), 1.0, 0.0).astype(jnp.bfloat16)
                    for y in range(n_blk)
                ],
                axis=1,
            )
        )
    pick = jnp.concatenate(picks, axis=0)
    for group in range(groups):
        rows = [divmod(group * n_blk + y, parts) for y in range(n_blk)]
        wide = jnp.concatenate([x_ref[part, win] for win, part in rows], axis=1)
        got = lax.dot_general(
            wide, pick, (((1,), (1,)), ((), ())), preferred_element_type=jnp.float32
        ).astype(jnp.bfloat16)
        for kind in range(kinds):
            out_ref[0, kind, group] = got[:, kind * chans : (kind + 1) * chans]


def select(flat, slots, partners, n_blk, kinds):
    parts, mine, nbins, chans = flat.shape
    groups = parts * mine // n_blk
    return pl.pallas_call(
        functools.partial(select_kernel, n_blk),
        grid=(n_blk,),
        out_shape=jax.ShapeDtypeStruct((n_blk, kinds, groups, nbins, chans), flat.dtype),
        in_specs=[
            pl.BlockSpec((1, chans), lambda d: (0, 0)),
            pl.BlockSpec(memory_space=pltpu.SMEM),
            pl.BlockSpec(flat.shape, lambda d: (0, 0, 0, 0)),
        ],
        out_specs=pl.BlockSpec((1, kinds, groups, nbins, chans), lambda d: (d, 0, 0, 0, 0)),
    )(slots, partners, flat)


def across(index, step, count):
    other, bit = index, 1
    while bit < count:
        if step & bit:
            other = flip(other, bit)
        bit *= 2
    return other


def fused_kernel(
    n, rounds, ahead, unroll, piece_ref, regroup_ref, turn_ref, table_ref, out_ref,
    got_ref, own_ref, stage_ref, right_ref, left_ref, side_ref, cross_ref, lag_ref, pad_ref,
    scale_ref, far_send, far_recv, stage_send, stage_recv, pass_send, pass_recv,
    own_send, own_recv, local_sem,
):
    blk = lax.axis_index("blk")
    win = lax.axis_index("win")
    groups = piece_ref.shape[2]

    def remote(src, dst, send, recv, to_blk, to_win):
        return pltpu.make_async_remote_copy(
            src_ref=src,
            dst_ref=dst,
            send_sem=send,
            recv_sem=recv,
            device_id={"blk": to_blk, "win": to_win},
            device_id_type=pl.DeviceIdType.MESH,
        )

    barrier = pltpu.get_barrier_semaphore()
    for step in range(1, n):
        for to_blk, to_win in ((across(blk, step, n), win), (blk, across(win, step, n))):
            pl.semaphore_signal(
                barrier,
                inc=1,
                device_id={"blk": to_blk, "win": to_win},
                device_id_type=pl.DeviceIdType.MESH,
            )

    def far(turn, step, group):
        dest = across(blk, step, n)
        return remote(
            piece_ref.at[dest, turn, group], got_ref.at[turn, blk, win, group],
            far_send.at[turn, step, group], far_recv.at[turn, step, group], dest, win,
        )

    def staged(step, group):
        dest = across(blk, step, n)
        return remote(
            piece_ref.at[dest, rounds, group], stage_ref.at[blk, group],
            stage_send.at[step, group], stage_recv.at[blk, group], dest, win,
        )

    def own(step, group):
        user = across(win, step, n)
        return remote(
            stage_ref.at[user, group], own_ref.at[win, group],
            own_send.at[step, group], own_recv.at[step, group], blk, user,
        )

    bits = []
    bit = n // 2
    while bit:
        bits.append(bit)
        bit //= 2
    passes = []
    held = [0]
    for over in bits:
        passes.extend((offset, over) for offset in held)
        held = held + [offset | over for offset in held]

    def passed(turn, step, group, offset, over):
        origin = across(blk, step, n)
        piece = got_ref.at[turn, origin, across(win, offset, n), group]
        source = piece_ref.at[blk, turn, group] if step == 0 and offset == 0 else piece
        mark = (offset | over) - 1
        return remote(
            source, piece, pass_send.at[turn, step, group, mark],
            pass_recv.at[turn, step, group, mark], blk, flip(win, over),
        )

    sends = []

    def go(copy):
        copy.start()
        sends.append(copy)

    keeps = [
        pltpu.make_async_copy(
            piece_ref.at[blk, turn], got_ref.at[turn, blk, win], local_sem.at[turn]
        )
        for turn in range(rounds)
    ]
    homes = [
        pltpu.make_async_copy(
            piece_ref.at[blk, rounds, group], stage_ref.at[blk, group], stage_recv.at[blk, group]
        )
        for group in range(groups)
    ]
    for keep in homes + keeps:
        keep.start()
    pl.semaphore_wait(barrier, 2 * (n - 1))
    steps = list(range(n - 1, 0, -1))
    waves = [(None, group) for group in range(groups)]
    waves += [(turn, group) for turn in range(rounds) for group in range(groups)]

    def launch(index):
        if index < len(waves):
            turn, group = waves[index]
            for step in steps:
                go(staged(step, group) if turn is None else far(turn, step, group))

    for index in range(ahead):
        launch(index)
    for turn in range(rounds):
        for group in range(groups):
            for offset, over in passes:
                if offset == 0:
                    go(passed(turn, 0, group, 0, over))

    waited = set()

    def arrive(turn, step, group, offset):
        if (turn, step, group, offset) in waited:
            return
        waited.add((turn, step, group, offset))
        if offset == 0:
            if step:
                far(turn, step, group).wait_recv()
        else:
            over = offset & -offset
            passed(turn, step, group, offset - over, over).wait_recv()

    def onward(turn, step, group, first):
        for offset, over in passes:
            if (offset == 0) == first:
                arrive(turn, step, group, offset)
                go(passed(turn, step, group, offset, over))

    nbins, chans = piece_ref.shape[3:]
    per_peer = chans // n
    depth = n * groups * n
    stride = left_ref.shape[0] // depth
    both = 2 * per_peer
    apart = both + 1
    nlags = out_ref.shape[1]
    pad = (pad_ref.shape[0] - stride) // 2

    def level_scale(power):
        place = lax.broadcasted_iota(jnp.int32, (nbins, chans), 0)
        count = 1 + jnp.minimum(place, half_band) + jnp.minimum(nbins - 1 - place, half_band)
        pad_ref[pl.ds(pad, nbins)] = power
        near = pad_ref[pl.ds(pad - half_band, nbins)]
        for offset in range(1 - half_band, half_band + 1):
            near = near + pad_ref[pl.ds(pad + offset, nbins)]
        return lax.rsqrt(near / (count.astype(jnp.float32) * (depth // 2)) + eps_power)

    def own_scale():
        for group in range(groups):
            for step in range(1, n):
                own(step, group).wait_recv()
        for copy in mine:
            copy.wait()
        mine.clear()
        pad_ref[...] = jnp.zeros_like(pad_ref)
        scale_ref[...] = jnp.zeros_like(scale_ref)

        def add(index, total):
            value = own_ref[index // groups, index % groups].astype(jnp.float32)
            return total + value * value

        power = lax.fori_loop(0, n * groups, add, jnp.zeros((nbins, chans), jnp.float32))
        total = power
        for y in range(1, n):
            total = total + pltpu.roll(power, y * per_peer, 1)
        scale_ref[rounds] = level_scale(total)

    def own_left():
        def one(index, carry):
            value = own_ref[index // groups, index % groups].astype(jnp.float32)
            white = (value * scale_ref[rounds]).astype(jnp.bfloat16)
            wide = jnp.dot(white, turn_ref[...], preferred_element_type=jnp.float32)
            for y in range(n):
                left_ref[pl.ds((index * n + y) * stride, nbins)] = wide[
                    :, y * chans : (y + 1) * chans
                ]
            return carry

        lax.fori_loop(0, n * groups, one, 0)

    def binwise(one, share, shares):
        full = nbins // unroll
        low, high = full * share // shares, full * (share + 1) // shares

        def some(index, carry):
            for offset in range(unroll):
                one(index * unroll + offset)
            return carry

        lax.fori_loop(low, high, some, 0)
        if share == shares - 1:
            for bin_index in range(full * unroll, nbins):
                one(bin_index)

    def own_side(share, shares):
        def one(bin_index):
            side = left_ref[pl.ds(bin_index, depth, stride)].T
            side_ref[bin_index] = side[:both].astype(jnp.bfloat16)

        binwise(one, share, shares)

    def regroup(turn, group):
        for step in range(n):
            for offset in held:
                arrive(turn, step, group, offset)
        if group == 0:
            keeps[turn].wait()

        def one(slot, carry):
            raw = jnp.concatenate([got_ref[turn, shard, slot, group] for shard in range(n)], axis=1)
            wide = jnp.dot(raw, regroup_ref[...], preferred_element_type=jnp.float32)
            power = scale_ref[turn]
            for y in range(n):
                part = wide[:, y * chans : (y + 1) * chans]
                right_ref[turn, pl.ds(((slot * groups + group) * n + y) * stride, nbins)] = part
                power = power + part * part
            scale_ref[turn] = power
            return carry

        lax.fori_loop(0, n, one, 0)

    def right_scale(turn):
        scale_ref[turn] = level_scale(scale_ref[turn])

    def cross(turn, share, shares):
        def one(bin_index):
            right = right_ref[turn, pl.ds(bin_index, depth, stride)].astype(jnp.bfloat16)
            value = jnp.dot(side_ref[bin_index], right, preferred_element_type=jnp.float32)
            scale = scale_ref[turn, pl.ds(bin_index, 1)]
            value = jnp.where(scale > 0.0, value * scale, 0.0)
            cross_ref[turn, pl.ds(bin_index * apart, both)] = value

        binwise(one, share, shares)

    def to_lags(turn, share, shares):
        batch = math.gcd(per_peer // shares, 4)
        count = per_peer // shares // batch

        def some(index, carry):
            for offset in range(batch):
                source = batch * index + offset
                total = None
                for part in range(2):
                    rows = cross_ref[turn, pl.ds(part * per_peer + source, nbins, apart)]
                    term = jnp.dot(
                        table_ref[part], rows.astype(jnp.bfloat16), preferred_element_type=jnp.float32
                    )
                    total = term if total is None else total + term
                lag_ref[turn, pl.ds(source, nlags, per_peer + 1)] = total
            return carry

        lax.fori_loop(count * share, count * (share + 1), some, 0)

    def settle(turn):
        for lag in range(nlags):
            out_ref[turn, lag] = lag_ref[turn, pl.ds(lag * (per_peer + 1), per_peer)].astype(
                out_ref.dtype
            )

    tasks = [(groups, own_scale), (groups, own_left)]
    shares = 4
    for share in range(shares):
        tasks.append((groups, functools.partial(own_side, share, shares)))
    for turn in range(rounds):
        first = groups * (turn + 1) + 2
        for group in range(groups):
            tasks.append((first + group, functools.partial(regroup, turn, group)))
        first += groups - 1
        tasks.append((first, functools.partial(right_scale, turn)))
        shares = 4 if turn < rounds - 1 else 1
        for share in range(shares):
            tasks.append((first, functools.partial(cross, turn, share, shares)))
        for share in range(shares):
            tasks.append((first, functools.partial(to_lags, turn, share, shares)))
        tasks.append((first, functools.partial(settle, turn)))

    def tick(index):
        if tasks and tasks[0][0] <= index:
            tasks.pop(0)[1]()

    mine = []
    late = []
    for index, (turn, group) in enumerate(waves):
        if turn is None:
            for step in range(1, n):
                source = across(blk, step, n)
                piece = stage_ref.at[source, group]
                pltpu.make_async_copy(piece, piece, stage_recv.at[source, group]).wait()
            piece = stage_ref.at[blk, group]
            pltpu.make_async_copy(piece, piece, stage_recv.at[blk, group]).wait()
            for step in steps:
                go(own(step, group))
            copy = pltpu.make_async_copy(
                stage_ref.at[win, group], own_ref.at[win, group], local_sem.at[rounds + group]
            )
            copy.start()
            mine.append(copy)
        else:
            for step in range(1, n):
                onward(turn, step, group, True)
        launch(index + ahead)
        for item in late:
            onward(*item, False)
        if turn is not None:
            for _ in range(3):
                tick(index)
        if turn is None:
            late = [(turn, 0, group) for turn in range(rounds)]
        else:
            late = [(turn, step, group) for step in range(1, n)]
    for item in late:
        onward(*item, False)
    while tasks:
        tasks.pop(0)[1]()
    for copy in sends:
        copy.wait_send()


def fused(pieces, n, rounds, windows):
    shape, dtype = pieces.shape[2:], pieces.dtype
    groups, nbins, chans = shape
    per_peer = chans // n
    depth = n * groups * n
    stride = (nbins + 7) // 8 * 8
    wide, turned = lane_spread(n, per_peer, chans)
    table = fixed_table(nbins, L, windows)
    vmem = pl.BlockSpec(memory_space=pltpu.VMEM)
    dma = pltpu.SemaphoreType.DMA
    return pl.pallas_call(
        functools.partial(fused_kernel, n, rounds, 2, 16),
        out_shape=jax.ShapeDtypeStruct((rounds, L, per_peer, chans), jnp.bfloat16),
        in_specs=[vmem] * 4,
        out_specs=vmem,
        scratch_shapes=[
            pltpu.VMEM((rounds, n, n, *shape), dtype),
            pltpu.VMEM((n, *shape), dtype),
            pltpu.VMEM((n, *shape), dtype),
            pltpu.VMEM((rounds, depth * stride, chans), jnp.float32),
            pltpu.VMEM((depth * stride, chans), jnp.float32),
            pltpu.VMEM((nbins, 2 * per_peer, depth), jnp.bfloat16),
            pltpu.VMEM((rounds, nbins * (2 * per_peer + 1), chans), jnp.float32),
            pltpu.VMEM((rounds, L * (per_peer + 1), chans), jnp.float32),
            pltpu.VMEM((stride + 16, chans), jnp.float32),
            pltpu.VMEM((rounds + 1, nbins, chans), jnp.float32),
            dma((rounds, n, groups)), dma((rounds, n, groups)), dma((n, groups)), dma((n, groups)),
            dma((rounds, n, groups, n - 1)), dma((rounds, n, groups, n - 1)),
            dma((n, groups)), dma((n, groups)), dma((rounds + groups,)),
        ],
        compiler_params=pltpu.CompilerParams(
            collective_id=1, has_side_effects=True, vmem_limit_bytes=48 * 2**20
        ),
    )(
        pieces, jnp.asarray(wide, jnp.bfloat16), jnp.asarray(turned, jnp.bfloat16),
        jnp.asarray(table, jnp.bfloat16),
    )


def lane_spread(n, per_peer, chans):
    regroup = np.zeros((n, n, per_peer, n, n, per_peer), np.float32)
    for shard in range(n):
        for y in range(n):
            for q in range(per_peer):
                regroup[shard, y, q, y, shard, q] = 1.0
    turned = np.zeros((n, per_peer, n, chans), np.float32)
    for y in range(n):
        for q in range(per_peer):
            turned[y, q, y, q] = 1.0
            part = y % 2
            turned[y + 1 - 2 * part, q, y, per_peer + q] = 1.0 if part == 0 else -1.0
    return regroup.reshape(n * chans, n * chans), turned.reshape(chans, n * chans)


def fixed_table(nbins, nlags, windows):
    samples = 2 * (nbins - 1)
    freq = np.arange(nbins)
    lags = np.arange(nlags) - (nlags - 1) // 2
    angle = 2.0 * np.pi / samples * (lags[:, None] * freq[None, :] % samples)
    weight = np.where((freq == 0) | (freq == nbins - 1), 1.0, 2.0) / np.sqrt(windows * samples)
    return np.stack([np.cos(angle) * weight, -np.sin(angle) * weight]).astype(np.float32)


def dense_body(spectra, channel_slot, partners):
    n = lax.axis_size("blk")
    parts, mine, chans, nbins = spectra.shape
    rounds = partners.shape[0]
    flat = spectra.transpose(0, 1, 3, 2)
    pieces = select(flat, channel_slot.reshape(1, chans), partners, n, rounds + 1)
    return fused(pieces, n, rounds, mine * n).transpose(0, 2, 1, 3)


def body(spectra, channel_slot, partners):
    n_blk = lax.axis_size("blk")
    rows = spectra.shape[0] * spectra.shape[1]
    fits = n_blk == lax.axis_size("win") and rows % n_blk == 0 and n_blk % spectra.shape[0] == 0
    if fits and 2 * spectra.shape[2] // n_blk <= spectra.shape[2]:
        return dense_body(spectra, channel_slot, partners)
    return plain_body(spectra, channel_slot, partners)


def solution(mesh):
    in_specs = (P(None, "win", ("groups", "blk"), None), P(("groups", "blk")), P())
    out_specs = P(None, ("groups", "blk", "win"), None, None)
    return jax.shard_map(body, mesh=mesh, in_specs=in_specs, out_specs=out_specs, check_vma=False)
```

```python
import functools
import math

import jax
import jax.numpy as jnp
import numpy as np
from jax import lax
from jax.experimental import pallas as pl
from jax.experimental.pallas import tpu as pltpu
from jax.sharding import PartitionSpec as P

L = 101
ROUNDS = 2


eps_power = 1e-06
half_band = 2
tile_rows = 8


def whiten_into(piece, store, n_win, rows):
    power = None
    for win in range(n_win):
        value_array = piece(win).astype(jnp.float32)
        part = jnp.sum(value_array * value_array, axis=0)
        power = part if power is None else power + part
    nbins = power.shape[1]
    padding = jnp.zeros((power.shape[0], half_band), jnp.float32)
    padded = jnp.concatenate([padding, power, padding], axis=1)
    total = padded[:, 0:nbins]
    for offset in range(1, 2 * half_band + 1):
        total = total + padded[:, offset : offset + nbins]
    place = lax.broadcasted_iota(jnp.int32, power.shape, 1)
    count = 1 + jnp.minimum(place, half_band) + jnp.minimum(nbins - 1 - place, half_band)
    level = total / (count.astype(jnp.float32) * (n_win * rows // 2))
    scale = lax.rsqrt(level + eps_power)
    for win in range(n_win):
        store(win, (piece(win).astype(jnp.float32) * scale).astype(jnp.bfloat16))


def lag_table(nbins, nlags, windows):
    samples = 2 * (nbins - 1)
    freq = jnp.arange(nbins, dtype=jnp.int32)
    lags = jnp.arange(nlags, dtype=jnp.int32) - (nlags - 1) // 2
    phase_index = freq[:, None] * lags[None, :] % samples
    angle = 2.0 * math.pi / samples * phase_index.astype(jnp.float32)
    weight = jnp.where((freq == 0) | (freq == nbins - 1), 1.0, 2.0).astype(jnp.float32)
    norm = 1.0 / math.sqrt(windows * samples)
    cos_part = weight[:, None] * jnp.cos(angle) * norm
    sin_part = -weight[:, None] * jnp.sin(angle) * norm
    return jnp.concatenate([cos_part, sin_part], axis=0)


def correlate(both, right, table):
    cross = jnp.einsum(
        "cwak,wbk->kcab", both, right, preferred_element_type=jnp.float32
    ).astype(jnp.bfloat16)
    return jnp.einsum(
        "kcab,ckl->lab", cross, table, preferred_element_type=jnp.float32
    ).astype(jnp.bfloat16)


def flip(index, bit):
    return index + bit - 2 * bit * ((index // bit) % 2)


def exchange_kernel(
    n_blk, n_win, rounds, pair_ref, own_ref, *refs
):
    right_refs = refs[:rounds]
    both_ref, got_ref, src_ref, pair_send, pair_recv = refs[rounds : rounds + 5]
    pass_send, pass_recv, own_send, own_recv, local_sem = refs[rounds + 5 :]
    blk = lax.axis_index("blk")
    win = lax.axis_index("win")
    per_share = n_blk // n_win
    barrier = pltpu.get_barrier_semaphore()
    for step in range(1, n_blk * n_win):
        other = (blk * n_win + win + step) % (n_blk * n_win)
        pl.semaphore_signal(
            barrier,
            inc=1,
            device_id={"blk": other // n_win, "win": other % n_win},
            device_id_type=pl.DeviceIdType.MESH,
        )
    pl.semaphore_wait(barrier, n_blk * n_win - 1)

    def remote(src, dst, send, recv, to_blk, to_win):
        return pltpu.make_async_remote_copy(
            src_ref=src,
            dst_ref=dst,
            send_sem=send,
            recv_sem=recv,
            device_id={"blk": to_blk, "win": to_win},
            device_id_type=pl.DeviceIdType.MESH,
        )

    bits = []
    bit = n_win // 2
    while bit:
        bits.append(bit)
        bit //= 2

    order = list(range(n_blk))

    def across(step):
        other, each = blk, 1
        while each < n_blk:
            if step & each:
                other = flip(other, each)
            each *= 2
        return other

    def direct(step):
        dest = across(step)
        return remote(
            pair_ref.at[:, :, dest], got_ref.at[:, win, :, blk],
            pair_send.at[step], pair_recv.at[step], dest, win,
        )

    user = blk // per_share
    place = blk % per_share

    def own(step):
        dest = across(step)
        return remote(
            own_ref.at[:, dest], src_ref.at[win, :, place],
            own_send.at[step], own_recv.at[place * n_win + win], dest, user,
        )

    def passed(step, offset, over):
        origin = across(step)
        slot = win
        for each in bits:
            if offset & each:
                slot = flip(slot, each)
        target = got_ref.at[:, slot, :, origin]
        source = pair_ref.at[:, :, blk] if step == 0 and offset == 0 else target
        mark = (offset | over) - 1
        return remote(
            source, target, pass_send.at[mark, step], pass_recv.at[mark, step], blk, flip(win, over)
        )

    rows = pair_ref.shape[1]
    half = rows // 2
    keep = pltpu.make_async_copy(
        pair_ref.at[:, :, blk], got_ref.at[:, win, :, blk], local_sem.at[0]
    )
    keep.start()
    is_user = user == win

    def own_keep():
        return pltpu.make_async_copy(
            own_ref.at[:, blk], src_ref.at[win, :, place], local_sem.at[1]
        )

    @pl.when(is_user)
    def _():
        own_keep().start()

    passes = []
    held = [0]
    for over in bits:
        passes.extend((offset, over) for offset in held)
        held = held + [offset | over for offset in held]

    sends = []
    for offset, over in passes:
        if offset == 0:
            copy = passed(0, 0, over)
            copy.start()
            sends.append(copy)
    for step in order[1:]:
        copy = direct(step)
        copy.start()
        sends.append(copy)
    for step in order[1:]:
        copy = own(step)
        copy.start()
        sends.append(copy)

    @pl.when(jnp.logical_not(is_user))
    def _():
        own(0).start()

    keep.wait()

    @pl.when(is_user)
    def _():
        own_keep().wait()

    waited = set()

    def arrive(step, offset):
        if (step, offset) in waited:
            return
        waited.add((step, offset))
        if offset == 0:
            if step:
                direct(step).wait_recv()
        else:
            over = offset & -offset
            passed(step, offset - over, over).wait_recv()

    def finish(step):
        for offset in held:
            arrive(step, offset)
        origin = across(step)

        for index in range(rounds):

            def store(peer, white):
                right_refs[index][pl.ds(peer * rows, rows), origin] = white

            whiten_into(lambda peer: got_ref[index, peer, :, origin], store, n_win, rows)

    for turn in range(n_blk + 1):
        if 1 <= turn < n_blk:
            step = order[turn]
            arrive(step, 0)
            for offset, over in passes:
                if offset == 0:
                    copy = passed(step, 0, over)
                    copy.start()
                    sends.append(copy)
        if turn >= 1:
            step = order[turn - 1]
            for offset, over in passes:
                if offset:
                    arrive(step, offset)
                    copy = passed(step, offset, over)
                    copy.start()
                    sends.append(copy)
        if turn >= 2:
            finish(order[turn - 2])
    finish(order[n_blk - 1])
    for local in range(per_share):
        for peer in range(n_win):
            here = jnp.logical_and(blk == win * per_share + local, win == peer)

            @pl.when(jnp.logical_not(here))
            def _():
                piece = src_ref.at[peer, :, local]
                remote(
                    piece, piece, own_send.at[0], own_recv.at[local * n_win + peer], blk, win
                ).wait_recv()

    def one_shard(local, carry):
        def store(peer, white):
            both_ref[0, pl.ds(peer * rows, rows), local] = white
            both_ref[1, pl.ds(peer * rows, half), local] = white[half:]
            both_ref[1, pl.ds(peer * rows + half, half), local] = -white[:half]

        whiten_into(lambda peer: src_ref[peer, :, local], store, n_win, rows)
        return carry

    lax.fori_loop(0, per_share, one_shard, 0)

    for copy in sends:
        copy.wait_send()

    @pl.when(jnp.logical_not(is_user))
    def _():
        own(0).wait_send()


def exchange(pair, own, n_blk, n_win):
    rounds, rows, _, per_peer, nbins = pair.shape
    per_share = n_blk // n_win
    dtype = pair.dtype
    anywhere = pl.BlockSpec(memory_space=pl.ANY)
    vmem = pl.BlockSpec(memory_space=pltpu.VMEM)
    depth = n_win * rows
    return pl.pallas_call(
        functools.partial(exchange_kernel, n_blk, n_win, rounds),
        out_shape=(
            *[jax.ShapeDtypeStruct((depth, n_blk, per_peer, nbins), dtype)] * rounds,
            jax.ShapeDtypeStruct((2, depth, per_share, per_peer, nbins), dtype),
        ),
        in_specs=[anywhere, anywhere],
        out_specs=(vmem,) * (rounds + 1),
        scratch_shapes=[
            pltpu.VMEM((rounds, n_win, rows, n_blk, per_peer, nbins), dtype),
            pltpu.VMEM((n_win, rows, per_share, per_peer, nbins), dtype),
            pltpu.SemaphoreType.DMA((n_blk,)),
            pltpu.SemaphoreType.DMA((n_blk,)),
            pltpu.SemaphoreType.DMA((n_win - 1, n_blk)),
            pltpu.SemaphoreType.DMA((n_win - 1, n_blk)),
            pltpu.SemaphoreType.DMA((n_blk,)),
            pltpu.SemaphoreType.DMA((n_blk,)),
            pltpu.SemaphoreType.DMA((2,)),
        ],
        compiler_params=pltpu.CompilerParams(collective_id=0, has_side_effects=True),
    )(pair, own)


def plain_body(spectra, channel_slot, partners):
    n_blk = lax.axis_size("blk")
    n_win = lax.axis_size("win")
    parts, mine, chans, nbins = spectra.shape
    rows = parts * mine
    per_peer = chans // n_blk
    here = lax.axis_index("blk")
    share = chans // n_win
    windows = mine * n_win
    flat = spectra.reshape(rows, chans, nbins)
    wanted = jnp.concatenate([partners, jnp.arange(n_blk, dtype=jnp.int32)[None]], axis=0)
    slots = (
        wanted[:, :, None] * chans
        + here * per_peer
        + jnp.arange(per_peer, dtype=jnp.int32)[None, None, :]
    )
    selector = (slots[..., None] == channel_slot).astype(jnp.bfloat16)
    pair = jnp.einsum(
        "tzqc,xcf->txzqf", selector[:ROUNDS], flat, preferred_element_type=jnp.float32
    ).astype(jnp.bfloat16)
    own = jnp.einsum(
        "zqc,xcf->xzqf", selector[ROUNDS], flat, preferred_element_type=jnp.float32
    ).astype(jnp.bfloat16)
    *right, both = exchange(pair, own, n_blk, n_win)
    right = [each.reshape(n_win * rows, chans, nbins) for each in right]
    both = both.reshape(2, n_win * rows, share, nbins)
    table = lag_table(nbins, L, windows).reshape(2, nbins, L).astype(jnp.bfloat16)
    results = [correlate(both, right[index], table) for index in range(ROUNDS)]
    return jnp.stack(results, axis=0).transpose(0, 2, 1, 3)


def select_kernel(n_blk, slots_ref, partners_ref, x_ref, out_ref):
    dest = pl.program_id(0)
    here = lax.axis_index("blk")
    parts, _, nbins, chans = x_ref.shape
    kinds, groups = out_ref.shape[1], out_ref.shape[2]
    per_peer = chans // n_blk
    row = lax.broadcasted_iota(jnp.int32, (chans, chans), 0)
    slots = slots_ref[...]
    picks = []
    for kind in range(kinds):
        block = dest if kind == kinds - 1 else partners_ref[kind, dest]
        hit = slots == block * chans + here * per_peer + row % per_peer
        picks.append(
            jnp.concatenate(
                [
                    jnp.where(hit & (row // per_peer == y), 1.0, 0.0).astype(jnp.bfloat16)
                    for y in range(n_blk)
                ],
                axis=1,
            )
        )
    pick = jnp.concatenate(picks, axis=0)
    for group in range(groups):
        rows = [divmod(group * n_blk + y, parts) for y in range(n_blk)]
        wide = jnp.concatenate([x_ref[part, win] for win, part in rows], axis=1)
        got = lax.dot_general(
            wide, pick, (((1,), (1,)), ((), ())), preferred_element_type=jnp.float32
        ).astype(jnp.bfloat16)
        for kind in range(kinds):
            out_ref[0, kind, group] = got[:, kind * chans : (kind + 1) * chans]


def select(flat, slots, partners, n_blk, kinds):
    parts, mine, nbins, chans = flat.shape
    groups = parts * mine // n_blk
    return pl.pallas_call(
        functools.partial(select_kernel, n_blk),
        grid=(n_blk,),
        out_shape=jax.ShapeDtypeStruct((n_blk, kinds, groups, nbins, chans), flat.dtype),
        in_specs=[
            pl.BlockSpec((1, chans), lambda d: (0, 0)),
            pl.BlockSpec(memory_space=pltpu.SMEM),
            pl.BlockSpec(flat.shape, lambda d: (0, 0, 0, 0)),
        ],
        out_specs=pl.BlockSpec((1, kinds, groups, nbins, chans), lambda d: (d, 0, 0, 0, 0)),
    )(slots, partners, flat)


def across(index, step, count):
    other, bit = index, 1
    while bit < count:
        if step & bit:
            other = flip(other, bit)
        bit *= 2
    return other


def fused_kernel(
    n, rounds, ahead, unroll, piece_ref, regroup_ref, turn_ref, table_ref, out_ref,
    got_ref, own_ref, stage_ref, right_ref, left_ref, side_ref, cross_ref, lag_ref, pad_ref,
    scale_ref, far_send, far_recv, stage_send, stage_recv, pass_send, pass_recv,
    own_send, own_recv, local_sem,
):
    blk = lax.axis_index("blk")
    win = lax.axis_index("win")
    groups = piece_ref.shape[2]

    def remote(src, dst, send, recv, to_blk, to_win):
        return pltpu.make_async_remote_copy(
            src_ref=src,
            dst_ref=dst,
            send_sem=send,
            recv_sem=recv,
            device_id={"blk": to_blk, "win": to_win},
            device_id_type=pl.DeviceIdType.MESH,
        )

    barrier = pltpu.get_barrier_semaphore()
    for step in range(1, n):
        for to_blk, to_win in ((across(blk, step, n), win), (blk, across(win, step, n))):
            pl.semaphore_signal(
                barrier,
                inc=1,
                device_id={"blk": to_blk, "win": to_win},
                device_id_type=pl.DeviceIdType.MESH,
            )

    def far(turn, step, group):
        dest = across(blk, step, n)
        return remote(
            piece_ref.at[dest, turn, group], got_ref.at[turn, blk, win, group],
            far_send.at[turn, step, group], far_recv.at[turn, step, group], dest, win,
        )

    def staged(step, group):
        dest = across(blk, step, n)
        return remote(
            piece_ref.at[dest, rounds, group], stage_ref.at[blk, group],
            stage_send.at[step, group], stage_recv.at[blk, group], dest, win,
        )

    def own(step, group):
        user = across(win, step, n)
        return remote(
            stage_ref.at[user, group], own_ref.at[win, group],
            own_send.at[step, group], own_recv.at[step, group], blk, user,
        )

    bits = []
    bit = n // 2
    while bit:
        bits.append(bit)
        bit //= 2
    passes = []
    held = [0]
    for over in bits:
        passes.extend((offset, over) for offset in held)
        held = held + [offset | over for offset in held]

    def passed(turn, step, group, offset, over):
        origin = across(blk, step, n)
        piece = got_ref.at[turn, origin, across(win, offset, n), group]
        source = piece_ref.at[blk, turn, group] if step == 0 and offset == 0 else piece
        mark = (offset | over) - 1
        return remote(
            source, piece, pass_send.at[turn, step, group, mark],
            pass_recv.at[turn, step, group, mark], blk, flip(win, over),
        )

    sends = []

    def go(copy):
        copy.start()
        sends.append(copy)

    keeps = [
        pltpu.make_async_copy(
            piece_ref.at[blk, turn], got_ref.at[turn, blk, win], local_sem.at[turn]
        )
        for turn in range(rounds)
    ]
    homes = [
        pltpu.make_async_copy(
            piece_ref.at[blk, rounds, group], stage_ref.at[blk, group], stage_recv.at[blk, group]
        )
        for group in range(groups)
    ]
    for keep in homes + keeps:
        keep.start()
    pl.semaphore_wait(barrier, 2 * (n - 1))
    steps = list(range(n - 1, 0, -1))
    waves = [(None, group) for group in range(groups)]
    waves += [(turn, group) for turn in range(rounds) for group in range(groups)]

    def launch(index):
        if index < len(waves):
            turn, group = waves[index]
            for step in steps:
                go(staged(step, group) if turn is None else far(turn, step, group))

    for index in range(ahead):
        launch(index)
    for turn in range(rounds):
        for group in range(groups):
            for offset, over in passes:
                if offset == 0:
                    go(passed(turn, 0, group, 0, over))

    waited = set()

    def arrive(turn, step, group, offset):
        if (turn, step, group, offset) in waited:
            return
        waited.add((turn, step, group, offset))
        if offset == 0:
            if step:
                far(turn, step, group).wait_recv()
        else:
            over = offset & -offset
            passed(turn, step, group, offset - over, over).wait_recv()

    def onward(turn, step, group, first):
        for offset, over in passes:
            if (offset == 0) == first:
                arrive(turn, step, group, offset)
                go(passed(turn, step, group, offset, over))

    nbins, chans = piece_ref.shape[3:]
    per_peer = chans // n
    depth = n * groups * n
    stride = left_ref.shape[0] // depth
    both = 2 * per_peer
    apart = both + 1
    nlags = out_ref.shape[1]
    pad = (pad_ref.shape[0] - stride) // 2

    def level_scale(power):
        place = lax.broadcasted_iota(jnp.int32, (nbins, chans), 0)
        count = 1 + jnp.minimum(place, half_band) + jnp.minimum(nbins - 1 - place, half_band)
        pad_ref[pl.ds(pad, nbins)] = power
        near = pad_ref[pl.ds(pad - half_band, nbins)]
        for offset in range(1 - half_band, half_band + 1):
            near = near + pad_ref[pl.ds(pad + offset, nbins)]
        return lax.rsqrt(near / (count.astype(jnp.float32) * (depth // 2)) + eps_power)

    def own_scale():
        for group in range(groups):
            for step in range(1, n):
                own(step, group).wait_recv()
        for copy in mine:
            copy.wait()
        mine.clear()
        pad_ref[...] = jnp.zeros_like(pad_ref)
        scale_ref[...] = jnp.zeros_like(scale_ref)

        def add(index, total):
            value = own_ref[index // groups, index % groups].astype(jnp.float32)
            return total + value * value

        power = lax.fori_loop(0, n * groups, add, jnp.zeros((nbins, chans), jnp.float32))
        total = power
        for y in range(1, n):
            total = total + pltpu.roll(power, y * per_peer, 1)
        scale_ref[rounds] = level_scale(total)

    def own_left():
        def one(index, carry):
            value = own_ref[index // groups, index % groups].astype(jnp.float32)
            white = (value * scale_ref[rounds]).astype(jnp.bfloat16)
            wide = jnp.dot(white, turn_ref[...], preferred_element_type=jnp.float32)
            for y in range(n):
                left_ref[pl.ds((index * n + y) * stride, nbins)] = wide[
                    :, y * chans : (y + 1) * chans
                ]
            return carry

        lax.fori_loop(0, n * groups, one, 0)

    def binwise(one, share, shares):
        full = nbins // unroll
        low, high = full * share // shares, full * (share + 1) // shares

        def some(index, carry):
            for offset in range(unroll):
                one(index * unroll + offset)
            return carry

        lax.fori_loop(low, high, some, 0)
        if share == shares - 1:
            for bin_index in range(full * unroll, nbins):
                one(bin_index)

    def own_side(share, shares):
        def one(bin_index):
            side = left_ref[pl.ds(bin_index, depth, stride)].T
            side_ref[bin_index] = side[:both].astype(jnp.bfloat16)

        binwise(one, share, shares)

    def regroup(turn, group):
        for step in range(n):
            for offset in held:
                arrive(turn, step, group, offset)
        if group == 0:
            keeps[turn].wait()

        def one(slot, carry):
            raw = jnp.concatenate([got_ref[turn, shard, slot, group] for shard in range(n)], axis=1)
            wide = jnp.dot(raw, regroup_ref[...], preferred_element_type=jnp.float32)
            power = scale_ref[turn]
            for y in range(n):
                part = wide[:, y * chans : (y + 1) * chans]
                right_ref[turn, pl.ds(((slot * groups + group) * n + y) * stride, nbins)] = part
                power = power + part * part
            scale_ref[turn] = power
            return carry

        lax.fori_loop(0, n, one, 0)

    def right_scale(turn):
        scale_ref[turn] = level_scale(scale_ref[turn])

    def cross(turn, share, shares):
        def one(bin_index):
            right = right_ref[turn, pl.ds(bin_index, depth, stride)].astype(jnp.bfloat16)
            value = jnp.dot(side_ref[bin_index], right, preferred_element_type=jnp.float32)
            scale = scale_ref[turn, pl.ds(bin_index, 1)]
            value = jnp.where(scale > 0.0, value * scale, 0.0)
            cross_ref[turn, pl.ds(bin_index * apart, both)] = value

        binwise(one, share, shares)

    def to_lags(turn, share, shares):
        batch = math.gcd(per_peer // shares, 8)
        count = per_peer // shares // batch

        def some(index, carry):
            for offset in range(batch):
                source = batch * index + offset
                total = None
                for part in range(2):
                    rows = cross_ref[turn, pl.ds(part * per_peer + source, nbins, apart)]
                    term = jnp.dot(
                        table_ref[part], rows.astype(jnp.bfloat16), preferred_element_type=jnp.float32
                    )
                    total = term if total is None else total + term
                lag_ref[turn, pl.ds(source, nlags, per_peer + 1)] = total
            return carry

        lax.fori_loop(count * share, count * (share + 1), some, 0)

    def settle(turn):
        for lag in range(nlags):
            out_ref[turn, lag] = lag_ref[turn, pl.ds(lag * (per_peer + 1), per_peer)].astype(
                out_ref.dtype
            )

    tasks = [(groups, own_scale), (groups, own_left)]
    shares = 4
    for share in range(shares):
        tasks.append((groups, functools.partial(own_side, share, shares)))
    for turn in range(rounds):
        first = groups * (turn + 1) + 2
        for group in range(groups):
            tasks.append((first + group, functools.partial(regroup, turn, group)))
        first += groups - 1
        tasks.append((first, functools.partial(right_scale, turn)))
        shares = 4 if turn < rounds - 1 else 1
        for share in range(shares):
            tasks.append((first, functools.partial(cross, turn, share, shares)))
        for share in range(shares):
            tasks.append((first, functools.partial(to_lags, turn, share, shares)))
        tasks.append((first, functools.partial(settle, turn)))

    def tick(index):
        if tasks and tasks[0][0] <= index:
            tasks.pop(0)[1]()

    mine = []
    late = []
    for index, (turn, group) in enumerate(waves):
        if turn is None:
            for step in range(1, n):
                source = across(blk, step, n)
                piece = stage_ref.at[source, group]
                pltpu.make_async_copy(piece, piece, stage_recv.at[source, group]).wait()
            piece = stage_ref.at[blk, group]
            pltpu.make_async_copy(piece, piece, stage_recv.at[blk, group]).wait()
            for step in steps:
                go(own(step, group))
            copy = pltpu.make_async_copy(
                stage_ref.at[win, group], own_ref.at[win, group], local_sem.at[rounds + group]
            )
            copy.start()
            mine.append(copy)
        else:
            for step in range(1, n):
                onward(turn, step, group, True)
        launch(index + ahead)
        for item in late:
            onward(*item, False)
        if turn is not None:
            for _ in range(3):
                tick(index)
        if turn is None:
            late = [(turn, 0, group) for turn in range(rounds)]
        else:
            late = [(turn, step, group) for step in range(1, n)]
    for item in late:
        onward(*item, False)
    while tasks:
        tasks.pop(0)[1]()
    for copy in sends:
        copy.wait_send()


def fused(pieces, n, rounds, windows):
    shape, dtype = pieces.shape[2:], pieces.dtype
    groups, nbins, chans = shape
    per_peer = chans // n
    depth = n * groups * n
    stride = (nbins + 7) // 8 * 8
    wide, turned = lane_spread(n, per_peer, chans)
    table = fixed_table(nbins, L, windows)
    vmem = pl.BlockSpec(memory_space=pltpu.VMEM)
    dma = pltpu.SemaphoreType.DMA
    return pl.pallas_call(
        functools.partial(fused_kernel, n, rounds, 2, 16),
        out_shape=jax.ShapeDtypeStruct((rounds, L, per_peer, chans), jnp.bfloat16),
        in_specs=[vmem] * 4,
        out_specs=vmem,
        scratch_shapes=[
            pltpu.VMEM((rounds, n, n, *shape), dtype),
            pltpu.VMEM((n, *shape), dtype),
            pltpu.VMEM((n, *shape), dtype),
            pltpu.VMEM((rounds, depth * stride, chans), jnp.float32),
            pltpu.VMEM((depth * stride, chans), jnp.float32),
            pltpu.VMEM((nbins, 2 * per_peer, depth), jnp.bfloat16),
            pltpu.VMEM((rounds, nbins * (2 * per_peer + 1), chans), jnp.float32),
            pltpu.VMEM((rounds, L * (per_peer + 1), chans), jnp.float32),
            pltpu.VMEM((stride + 16, chans), jnp.float32),
            pltpu.VMEM((rounds + 1, nbins, chans), jnp.float32),
            dma((rounds, n, groups)), dma((rounds, n, groups)), dma((n, groups)), dma((n, groups)),
            dma((rounds, n, groups, n - 1)), dma((rounds, n, groups, n - 1)),
            dma((n, groups)), dma((n, groups)), dma((rounds + groups,)),
        ],
        compiler_params=pltpu.CompilerParams(
            collective_id=1, has_side_effects=True, vmem_limit_bytes=48 * 2**20
        ),
    )(
        pieces, jnp.asarray(wide, jnp.bfloat16), jnp.asarray(turned, jnp.bfloat16),
        jnp.asarray(table, jnp.bfloat16),
    )


def lane_spread(n, per_peer, chans):
    regroup = np.zeros((n, n, per_peer, n, n, per_peer), np.float32)
    for shard in range(n):
        for y in range(n):
            for q in range(per_peer):
                regroup[shard, y, q, y, shard, q] = 1.0
    turned = np.zeros((n, per_peer, n, chans), np.float32)
    for y in range(n):
        for q in range(per_peer):
            turned[y, q, y, q] = 1.0
            part = y % 2
            turned[y + 1 - 2 * part, q, y, per_peer + q] = 1.0 if part == 0 else -1.0
    return regroup.reshape(n * chans, n * chans), turned.reshape(chans, n * chans)


def fixed_table(nbins, nlags, windows):
    samples = 2 * (nbins - 1)
    freq = np.arange(nbins)
    lags = np.arange(nlags) - (nlags - 1) // 2
    angle = 2.0 * np.pi / samples * (lags[:, None] * freq[None, :] % samples)
    weight = np.where((freq == 0) | (freq == nbins - 1), 1.0, 2.0) / np.sqrt(windows * samples)
    return np.stack([np.cos(angle) * weight, -np.sin(angle) * weight]).astype(np.float32)


def dense_body(spectra, channel_slot, partners):
    n = lax.axis_size("blk")
    parts, mine, chans, nbins = spectra.shape
    rounds = partners.shape[0]
    flat = spectra.transpose(0, 1, 3, 2)
    pieces = select(flat, channel_slot.reshape(1, chans), partners, n, rounds + 1)
    return fused(pieces, n, rounds, mine * n).transpose(0, 2, 1, 3)


def body(spectra, channel_slot, partners):
    n_blk = lax.axis_size("blk")
    rows = spectra.shape[0] * spectra.shape[1]
    fits = n_blk == lax.axis_size("win") and rows % n_blk == 0 and n_blk % spectra.shape[0] == 0
    if fits and 2 * spectra.shape[2] // n_blk <= spectra.shape[2]:
        return dense_body(spectra, channel_slot, partners)
    return plain_body(spectra, channel_slot, partners)


def solution(mesh):
    in_specs = (P(None, "win", ("groups", "blk"), None), P(("groups", "blk")), P())
    out_specs = P(None, ("groups", "blk", "win"), None, None)
    return jax.shard_map(body, mesh=mesh, in_specs=in_specs, out_specs=out_specs, check_vma=False)
```
